32 devices in a mesh: blk: 16 (over z, y, x), slab: 2 (over core).
Axes of the slice: x: 2, y: 2, z: 4, core: 2. Of those that a mesh axis runs over, the one named last changes fastest.
Arguments:
- sinogram: bfloat16 [32, 8, 2048], P('blk', 'slab'), parts along dimension 1, may hold values from -6 to 6
- jitter: bfloat16 [32], P('blk'), may hold values from -0.29882812 to 0.29882812
- shift: int32 [32], replicated, may hold values from -8 to 8
Outputs:
- image: float32 [32, 8, 2048], P('blk', 'slab'), parts along dimension 1
The draws below stay inside these ranges and needn't reach their ends.
There are 2 independent parts, one for each index of `slab`. The reference program is written for one: setup_inputs(seed, part) draws one part's arguments, and reference() takes and returns one part's arrays. A program takes and returns all parts, laid end to end along the dimension named above; an argument that names none is the same for every part. Nothing has to cross between parts.
All inputs are finite; a program needn't handle non-finite values.
Results may differ from the reference program's by a relative error of at most 0.0055.
Values may be sent and summed in bfloat16 or wider, within the bound.
A program may use at most 64 MiB of HBM per device.

```python
import math
import jax
import jax.numpy as jnp
from jax import lax

BINS = 2048
SLICES = 4
ANGLES = 32
NROWS = 32


def place_ends(array, rng, smallest, top_value):
    index_at = [jax.random.randint(jax.random.fold_in(rng, axis), (), 0, length) for axis, length in enumerate(array.shape)]
    main_axis = array.shape.index(max(array.shape))
    beside = index_at[:main_axis] + [(index_at[main_axis] + 1) % array.shape[main_axis]] + index_at[main_axis + 1:]
    return array.at[tuple(index_at)].set(smallest).at[tuple(beside)].set(top_value)


def block_scale(rng, shape, split, smallest, high):
    def one(dim, shards_of):
        heights = jax.random.uniform(jax.random.fold_in(jax.random.fold_in(rng, 6), dim), (shards_of,), jnp.float32, smallest / len(split), high / len(split))
        return jnp.repeat(jnp.exp(heights), shape[dim] // shards_of).reshape((-1,) + (1,) * (len(shape) - dim - 1))

    level = one(*split[0])
    for cut in split[1:]:
        level = level * one(*cut)
    return level


def bell_draw(key, shape, deviation, most, pieces=(), held_as=jnp.bfloat16):
    entries = deviation * jax.random.normal(key, shape, jnp.float32)
    if pieces:
        entries = entries * block_scale(key, shape, pieces, -0.22, 0.18)
    return jnp.clip(entries, -most, most).astype(held_as)


def setup_inputs(seed: int = 0, part: int = 0) -> dict:
    splits = jax.random.split(jax.random.key(seed), 4)
    part_keys = jax.random.split(jax.random.fold_in(splits[3], part), 4)
    return {
        "sinogram": bell_draw(part_keys[0], (ANGLES, SLICES, BINS), 1.0, 6.0, ((0, 16),)),
        "jitter": jnp.clip(jax.random.uniform(splits[1], (ANGLES,), jnp.float32, -0.29882812, 0.29882812) * block_scale(splits[1], (ANGLES,), ((0, 16),), -0.4, 0.0), -0.29882812, 0.29882812).astype(jnp.bfloat16),
        "shift": place_ends(jax.random.randint(splits[2], (ANGLES,), -8, 9), jax.random.fold_in(splits[2], 1), -8, 8).astype(jnp.int32),
    }


def ramp_matrix(bins):
    offsets = jnp.arange(bins, dtype=jnp.int32)[None, :] - jnp.arange(bins, dtype=jnp.int32)[:, None]
    safe = jnp.where(offsets == 0, 1, offsets).astype(jnp.float32)
    odd_part = jnp.where(offsets % 2 != 0, -1.0 / (math.pi ** 2 * safe * safe), jnp.float32(0.0))
    kernel = jnp.where(offsets == 0, jnp.float32(0.25), odd_part)
    return kernel.astype(jnp.bfloat16)

def reference(sinogram, jitter, shift):
    ramp = ramp_matrix(BINS)
    jit_vals = jitter.astype(jnp.float32)
    weight = (1.0 + (jnp.roll(jit_vals, -1) - jnp.roll(jit_vals, 1)) * 1.5) * (4.0 / math.sqrt(ANGLES))
    flat = jnp.dot(sinogram.reshape(ANGLES * SLICES, BINS), ramp, preferred_element_type=jnp.float32)
    filtered = (flat.reshape(ANGLES, SLICES, BINS) * weight[:, None, None]).astype(jnp.bfloat16)
    padding = BINS // 4 + 192
    padded = jnp.pad(filtered, ((0, 0), (0, 0), (padding, padding))).astype(jnp.float32)
    theta = (jnp.arange(ANGLES, dtype=jnp.float32) + jit_vals) * math.pi / ANGLES
    cosine = jnp.cos(theta)
    sine_part = jnp.sin(theta)
    center_bin = (BINS - 1) / 2 + shift.astype(jnp.float32)
    coords_x = jnp.arange(BINS, dtype=jnp.float32) - (BINS - 1) / 2

    def one_row(row):
        row_pos = row.astype(jnp.float32) - (NROWS - 1) / 2
        coords = coords_x[None, :] * cosine[:, None] + row_pos * sine_part[:, None] + center_bin[:, None]
        lower = jnp.floor(coords)
        upper = lower + 1.0
        w_lower = jnp.maximum(0.0, 1.0 - jnp.abs(lower - coords)).astype(jnp.bfloat16).astype(jnp.float32)
        w_upper = jnp.maximum(0.0, 1.0 - jnp.abs(upper - coords)).astype(jnp.bfloat16).astype(jnp.float32)
        low_idx = lower.astype(jnp.int32) + padding
        idx_lo = jnp.broadcast_to(low_idx[:, None, :], (ANGLES, SLICES, BINS))
        f_lower = jnp.take_along_axis(padded, idx_lo, axis=2)
        f_upper = jnp.take_along_axis(padded, idx_lo + 1, axis=2)
        return lax.optimization_barrier(jnp.sum(f_lower * w_lower[:, None, :] + f_upper * w_upper[:, None, :], axis=0))
    return lax.map(one_row, jnp.arange(NROWS, dtype=jnp.int32))
```

```python
import functools
import math

import jax
import jax.numpy as jnp
import numpy as np
from jax import lax
from jax.experimental import pallas as pl
from jax.experimental.pallas import tpu as pltpu
from jax.sharding import PartitionSpec as P

LANES = 128
SUBS = 8
BLOCK = 256
PLANE = 4
MESH = pl.DeviceIdType.MESH


def ramp_slab(bins):
    span = 2 * bins - BLOCK
    offsets = (
        np.arange(span, dtype=np.int32)[None, :]
        - np.int32(bins - BLOCK)
        - np.arange(BLOCK, dtype=np.int32)[:, None]
    )
    safe = np.where(offsets == 0, 1, offsets).astype(np.float32)
    odd_part = np.where(
        offsets % 2 != 0, np.float32(-1.0) / (np.float32(math.pi**2) * safe * safe), np.float32(0)
    )
    return np.where(offsets == 0, np.float32(0.25), odd_part).astype(jnp.bfloat16)


def kernel(
    width,
    jit_ref,
    shift_ref,
    sino_ref,
    slab_hbm,
    out_ref,
    slab,
    chunks,
    jmsg,
    jall,
    pvec,
    psm,
    fval,
    fdif,
    acc,
    lsem,
    sj,
    rj,
    sz,
    rz,
    sx,
    rx,
    sy,
    ry,
    sd,
    rd,
):
    me = lax.axis_index("blk")
    ang_dev, slices, bins = sino_ref.shape
    rows_dev = out_ref.shape[0]
    angles = width * ang_dev
    nrows = width * rows_dev
    nblocks = bins // LANES
    ntiles = fval.shape[1]
    depth = width // PLANE
    px, py = me % 2, (me // 2) % 2
    xpeer = me + 1 - 2 * px
    ypeer = me + 2 - 4 * py
    diag = me + 1 - 2 * px + 2 - 4 * py

    def remote(src, dst, send, recv, dev):
        return pltpu.make_async_remote_copy(
            src_ref=src,
            dst_ref=dst,
            send_sem=send,
            recv_sem=recv,
            device_id={"blk": dev},
            device_id_type=MESH,
        )

    def at(dev, k):
        return (dev + width - PLANE * k) % width

    def zcopy(k):
        return remote(
            chunks.at[me], chunks.at[me], sz.at[k], rz.at[k], (me + PLANE * k) % width
        )

    def xcopy(k):
        c = at(me, k)
        return remote(chunks.at[c], chunks.at[c], sx.at[k], rx.at[k], xpeer)

    def ycopy(k):
        c = at(me, k)
        return remote(chunks.at[c], chunks.at[c], sy.at[k], ry.at[k], ypeer)

    def relay_x(k):
        c = at(xpeer, k)
        return remote(
            chunks.at[c, 0], chunks.at[c, 0], sd.at[0, k], rd.at[0, k], ypeer
        )

    def relay_y(k):
        c = at(ypeer, k)
        return remote(
            chunks.at[c, 1], chunks.at[c, 1], sd.at[1, k], rd.at[1, k], xpeer
        )

    def jcopy(i):
        return remote(jmsg, jall.at[me], sj.at[i], rj.at[i], (me + i) % width)

    barrier = pltpu.get_barrier_semaphore()

    @pl.loop(1, width)
    def _(i):
        pl.semaphore_signal(
            barrier, inc=1, device_id={"blk": (me + i) % width}, device_id_type=MESH
        )

    load = pltpu.make_async_copy(slab_hbm, slab, lsem.at[0])
    load.start()

    lane = lax.broadcasted_iota(jnp.int32, (SUBS, LANES), 1)
    sub = lax.broadcasted_iota(jnp.int32, (SUBS, LANES), 0)
    lanef = lane.astype(jnp.float32)
    mine = (lane % angles) - me * ang_dev
    msg = jnp.zeros((SUBS, LANES), jnp.float32)
    for i in range(ang_dev):
        msg = jnp.where(mine == i, jit_ref[i], msg)
    jmsg[...] = msg
    jall[me] = msg
    zero = jnp.zeros((SUBS, LANES), jnp.float32)
    for i in range(ang_dev):
        for t in [0] + list(range(nblocks + 1, ntiles)):
            fval[i, t] = zero
            fdif[i, t] = zero
    for b in range(nblocks):
        acc[b] = zero

    nb = bins // BLOCK
    flat = jnp.concatenate(
        [sino_ref[i].astype(jnp.float32) for i in range(ang_dev)], axis=0
    )
    lhs = jnp.concatenate(
        [flat[:, i * BLOCK : (i + 1) * BLOCK] for i in range(nb)], axis=0
    ).astype(jnp.bfloat16)
    load.wait()
    total = [None] * nb
    for d in range(2 * nb - 1):
        prod = jnp.dot(
            lhs, slab[:, d * BLOCK : (d + 1) * BLOCK], preferred_element_type=jnp.float32
        )
        for i in range(nb):
            j = d - (nb - 1) + i
            if 0 <= j < nb:
                piece = prod[i * SUBS : (i + 1) * SUBS]
                total[j] = piece if total[j] is None else total[j] + piece
    row = jnp.concatenate(total, axis=1)
    quarter = bins // 4
    for h in range(2):
        chunks[me, h] = jnp.concatenate(
            [row[:, (2 * h + q) * quarter : (2 * h + q + 1) * quarter] for q in range(2)], axis=0
        ).astype(jnp.bfloat16)

    pl.semaphore_wait(barrier, width - 1)

    @pl.loop(1, width)
    def _(i):
        jcopy(i).start()

    @pl.loop(1, depth)
    def _(k):
        zcopy(k).start()

    xcopy(0).start()
    ycopy(0).start()

    @pl.loop(1, width)
    def _(i):
        jcopy(i).wait()

    jit = jall[0]
    for i in range(1, width):
        jit = jit + jall[i]
    ahead = pltpu.roll(jit, LANES - 1, 1)
    behind = pltpu.roll(jit, 1, 1)
    weight = (1.0 + (ahead - behind) * 1.5) * (4.0 / math.sqrt(angles))
    theta = ((lane % angles).astype(jnp.float32) + jit) * math.pi / angles
    pvec[...] = jnp.where(
        sub == 0, jnp.cos(theta), jnp.where(sub == 1, jnp.sin(theta), weight)
    )
    move = pltpu.make_async_copy(pvec, psm, lsem.at[1])
    move.start()
    move.wait()

    half = (bins - 1) / 2
    first_row = (me * rows_dev).astype(jnp.float32) - (nrows - 1) / 2
    rowf = (sub // slices).astype(jnp.float32) + first_row
    low_half = sub < slices

    def project(chunk):
        after = [None] * ang_dev
        wts = [psm[2, chunk * ang_dev + i] for i in range(ang_dev)]
        for t in range(nblocks - 1, -2, -1):
            if t >= 0:
                h, q, k = t // (nblocks // 2), (t // (nblocks // 4)) % 2, t % (nblocks // 4)
                tile = chunks[
                    chunk, h, q * SUBS : (q + 1) * SUBS, k * LANES : (k + 1) * LANES
                ].astype(jnp.float32)
                turned = pltpu.roll(tile, slices, 0)
                pair = [
                    jnp.where(low_half, tile, turned) * wts[0],
                    jnp.where(low_half, turned, tile) * wts[1],
                ]
            else:
                pair = [zero] * ang_dev
            for i in range(ang_dev):
                rolled = pltpu.roll(pair[i], LANES - 1, 1)
                nxt = zero if after[i] is None else after[i]
                fdif[i, t + 1] = jnp.where(lane == LANES - 1, nxt, rolled) - pair[i]
                if t >= 0:
                    fval[i, t + 1] = pair[i]
                after[i] = rolled
        for i in range(ang_dev):
            a = chunk * ang_dev + i
            cosine = psm[0, a]
            sine = psm[1, a]
            center = half + shift_ref[a].astype(jnp.float32)
            ramp = lanef * cosine + rowf * sine
            least = jnp.minimum(cosine * (LANES - 1), 0.0) + jnp.minimum(
                first_row * sine, (first_row + (rows_dev - 1)) * sine
            )
            for b in range(nblocks):
                base = (b * LANES - half) * cosine + center + LANES
                low = (base + least - 0.25).astype(jnp.int32) // LANES
                low = jnp.minimum(jnp.maximum(low, 0), ntiles - 2)
                u = ramp + (base - (low * LANES).astype(jnp.float32))
                bin_lo = u.astype(jnp.int32)
                frac = u - bin_lo.astype(jnp.float32)
                where = jnp.bitwise_and(bin_lo, LANES - 1)
                first = bin_lo < LANES

                def pick(ref):
                    return jnp.where(
                        first,
                        jnp.take_along_axis(ref[i, low], where, axis=1, mode="promise_in_bounds"),
                        jnp.take_along_axis(
                            ref[i, low + 1], where, axis=1, mode="promise_in_bounds"
                        ),
                    )

                acc[b] += pick(fval) + frac * pick(fdif)

    def relay(k):
        xcopy(k).wait_recv()
        relay_x(k).start()
        ycopy(k).wait_recv()
        relay_y(k).start()

    def corner(k):
        relay_x(k).wait_recv()
        relay_y(k).wait_recv()
        project(at(diag, k))

    project(me)
    relay(0)

    @pl.loop(1, depth)
    def _(k):
        zcopy(k).wait_recv()
        xcopy(k).start()
        ycopy(k).start()
        project(at(xpeer, k - 1))
        project(at(ypeer, k - 1))
        project(at(me, k))
        relay(k)
        corner(k - 1)

    project(at(xpeer, depth - 1))
    project(at(ypeer, depth - 1))
    corner(depth - 1)

    for b in range(nblocks):
        done = acc[b]
        for r in range(rows_dev):
            out_ref[r, :, b * LANES : (b + 1) * LANES] = done[r * slices : (r + 1) * slices]

    @pl.loop(0, depth)
    def _(k):
        xcopy(k).wait_send()
        ycopy(k).wait_send()
        relay_x(k).wait_send()
        relay_y(k).wait_send()

    @pl.loop(1, depth)
    def _(k):
        zcopy(k).wait_send()


def body(sinogram, jitter, shift):
    width = lax.axis_size("blk")
    ang_dev, slices, bins = sinogram.shape
    angles = shift.shape[0]
    rows_dev = SUBS // slices
    assert ang_dev == 2 and ang_dev * slices == SUBS and LANES % angles == 0
    assert width % PLANE == 0 and bins % (2 * BLOCK) == 0
    depth = width // PLANE
    ntiles = bins // LANES + 3
    vmem = pl.BlockSpec(memory_space=pltpu.VMEM)
    smem = pl.BlockSpec(memory_space=pltpu.SMEM)
    dma = pltpu.SemaphoreType.DMA
    slab = jnp.asarray(ramp_slab(bins))
    return pl.pallas_call(
        functools.partial(kernel, width),
        out_shape=jax.ShapeDtypeStruct((rows_dev, slices, bins), jnp.float32),
        in_specs=[smem, smem, vmem, pl.BlockSpec(memory_space=pl.ANY)],
        out_specs=vmem,
        scratch_shapes=[
            pltpu.VMEM(slab.shape, jnp.bfloat16),
            pltpu.VMEM((width, 2, 2 * SUBS, bins // 4), jnp.bfloat16),
            pltpu.VMEM((SUBS, LANES), jnp.float32),
            pltpu.VMEM((width, SUBS, LANES), jnp.float32),
            pltpu.VMEM((SUBS, LANES), jnp.float32),
            pltpu.SMEM((SUBS, LANES), jnp.float32),
            pltpu.VMEM((ang_dev, ntiles, SUBS, LANES), jnp.float32),
            pltpu.VMEM((ang_dev, ntiles, SUBS, LANES), jnp.float32),
            pltpu.VMEM((bins // LANES, SUBS, LANES), jnp.float32),
            dma((2,)),
            dma((width,)),
            dma((width,)),
            dma((depth,)),
            dma((depth,)),
            dma((depth,)),
            dma((depth,)),
            dma((depth,)),
            dma((depth,)),
            dma((2, depth)),
            dma((2, depth)),
        ],
        compiler_params=pltpu.CompilerParams(collective_id=0, has_side_effects=True),
    )(jitter.astype(jnp.float32), shift, sinogram, slab)


def solution(mesh):
    in_specs = (P("blk", "slab", None), P("blk"), P())
    out_specs = P("blk", "slab", None)
    return jax.shard_map(body, mesh=mesh, in_specs=in_specs, out_specs=out_specs, check_vma=False)
```

```python
import functools
import math

import jax
import jax.numpy as jnp
import numpy as np
from jax import lax
from jax.experimental import pallas as pl
from jax.experimental.pallas import tpu as pltpu
from jax.sharding import PartitionSpec as P

LANES = 128
SUBS = 8
BLOCK = 256
PLANE = 4
MESH = pl.DeviceIdType.MESH


def ramp_slab(bins):
    span = 2 * bins - BLOCK
    offsets = (
        np.arange(span, dtype=np.int32)[None, :]
        - np.int32(bins - BLOCK)
        - np.arange(BLOCK, dtype=np.int32)[:, None]
    )
    safe = np.where(offsets == 0, 1, offsets).astype(np.float32)
    odd_part = np.where(
        offsets % 2 != 0, np.float32(-1.0) / (np.float32(math.pi**2) * safe * safe), np.float32(0)
    )
    return np.where(offsets == 0, np.float32(0.25), odd_part).astype(jnp.bfloat16)


def kernel(
    width,
    jit_ref,
    shift_ref,
    sino_ref,
    slab_hbm,
    out_ref,
    slab,
    chunks,
    jmsg,
    jall,
    pvec,
    psm,
    fval,
    fdif,
    acc,
    lsem,
    sj,
    rj,
    sz,
    rz,
    sx,
    rx,
    sy,
    ry,
    sd,
    rd,
):
    me = lax.axis_index("blk")
    ang_dev, slices, bins = sino_ref.shape
    rows_dev = out_ref.shape[0]
    angles = width * ang_dev
    nrows = width * rows_dev
    nblocks = bins // LANES
    ntiles = fval.shape[1]
    depth = width // PLANE
    px, py = me % 2, (me // 2) % 2
    xpeer = me + 1 - 2 * px
    ypeer = me + 2 - 4 * py
    diag = me + 1 - 2 * px + 2 - 4 * py

    def remote(src, dst, send, recv, dev):
        return pltpu.make_async_remote_copy(
            src_ref=src,
            dst_ref=dst,
            send_sem=send,
            recv_sem=recv,
            device_id={"blk": dev},
            device_id_type=MESH,
        )

    def at(dev, k):
        return (dev + width - PLANE * k) % width

    def zcopy(k):
        return remote(
            chunks.at[me], chunks.at[me], sz.at[k], rz.at[k], (me + PLANE * k) % width
        )

    def xcopy(k):
        c = at(me, k)
        return remote(chunks.at[c], chunks.at[c], sx.at[k], rx.at[k], xpeer)

    def ycopy(k):
        c = at(me, k)
        return remote(chunks.at[c], chunks.at[c], sy.at[k], ry.at[k], ypeer)

    def relay_x(k):
        c = at(xpeer, k)
        return remote(
            chunks.at[c, 0], chunks.at[c, 0], sd.at[0, k], rd.at[0, k], ypeer
        )

    def relay_y(k):
        c = at(ypeer, k)
        return remote(
            chunks.at[c, 1], chunks.at[c, 1], sd.at[1, k], rd.at[1, k], xpeer
        )

    def jcopy(i):
        return remote(jmsg, jall.at[me], sj.at[i], rj.at[i], (me + i) % width)

    def relay(k):
        xcopy(k).wait_recv()
        relay_x(k).start()
        ycopy(k).wait_recv()
        relay_y(k).start()

    barrier = pltpu.get_barrier_semaphore()

    @pl.loop(1, width)
    def _(i):
        pl.semaphore_signal(
            barrier, inc=1, device_id={"blk": (me + i) % width}, device_id_type=MESH
        )

    load = pltpu.make_async_copy(slab_hbm, slab, lsem.at[0])
    load.start()

    lane = lax.broadcasted_iota(jnp.int32, (SUBS, LANES), 1)
    sub = lax.broadcasted_iota(jnp.int32, (SUBS, LANES), 0)
    lanef = lane.astype(jnp.float32)
    mine = (lane % angles) - me * ang_dev
    msg = jnp.zeros((SUBS, LANES), jnp.float32)
    for i in range(ang_dev):
        msg = jnp.where(mine == i, jit_ref[0:1, i : i + 1].astype(jnp.float32), msg)
    jmsg[...] = msg
    jall[me] = msg
    zero = jnp.zeros((SUBS, LANES), jnp.float32)
    for i in range(ang_dev):
        for t in [0] + list(range(nblocks + 1, ntiles)):
            fval[i, t] = zero
            fdif[i, t] = zero
    for b in range(nblocks):
        acc[b] = zero

    nb = bins // BLOCK
    flat = jnp.concatenate(
        [sino_ref[i].astype(jnp.float32) for i in range(ang_dev)], axis=0
    )
    lhs = jnp.concatenate(
        [flat[:, i * BLOCK : (i + 1) * BLOCK] for i in range(nb)], axis=0
    ).astype(jnp.bfloat16)
    load.wait()
    total = [None] * nb
    for d in range(2 * nb - 1):
        prod = jnp.dot(
            lhs, slab[:, d * BLOCK : (d + 1) * BLOCK], preferred_element_type=jnp.float32
        )
        for i in range(nb):
            j = d - (nb - 1) + i
            if 0 <= j < nb:
                piece = prod[i * SUBS : (i + 1) * SUBS]
                total[j] = piece if total[j] is None else total[j] + piece
    row = jnp.concatenate(total, axis=1)
    quarter = bins // 4
    for h in range(2):
        chunks[me, h] = jnp.concatenate(
            [row[:, (2 * h + q) * quarter : (2 * h + q + 1) * quarter] for q in range(2)], axis=0
        ).astype(jnp.bfloat16)

    pl.semaphore_wait(barrier, width - 1)

    @pl.loop(1, width)
    def _(i):
        jcopy(i).start()

    @pl.loop(1, depth)
    def _(k):
        zcopy(k).start()

    xcopy(0).start()
    ycopy(0).start()

    relay(0)

    @pl.loop(1, depth)
    def _(k):
        zcopy(k).wait_recv()
        xcopy(k).start()
        ycopy(k).start()

    @pl.loop(1, width)
    def _(i):
        jcopy(i).wait()

    jit = jall[0]
    for i in range(1, width):
        jit = jit + jall[i]
    ahead = pltpu.roll(jit, LANES - 1, 1)
    behind = pltpu.roll(jit, 1, 1)
    weight = (1.0 + (ahead - behind) * 1.5) * (4.0 / math.sqrt(angles))
    theta = ((lane % angles).astype(jnp.float32) + jit) * math.pi / angles
    pvec[...] = jnp.where(
        sub == 0, jnp.cos(theta), jnp.where(sub == 1, jnp.sin(theta), weight)
    )
    move = pltpu.make_async_copy(pvec, psm, lsem.at[1])
    move.start()
    move.wait()

    half = (bins - 1) / 2
    first_row = (me * rows_dev).astype(jnp.float32) - (nrows - 1) / 2
    rowf = (sub // slices).astype(jnp.float32) + first_row
    low_half = sub < slices

    def project(chunk):
        after = [None] * ang_dev
        wts = [psm[2, chunk * ang_dev + i] for i in range(ang_dev)]
        for t in range(nblocks - 1, -2, -1):
            if t >= 0:
                h, q, k = t // (nblocks // 2), (t // (nblocks // 4)) % 2, t % (nblocks // 4)
                tile = chunks[
                    chunk, h, q * SUBS : (q + 1) * SUBS, k * LANES : (k + 1) * LANES
                ].astype(jnp.float32)
                turned = pltpu.roll(tile, slices, 0)
                pair = [
                    jnp.where(low_half, tile, turned) * wts[0],
                    jnp.where(low_half, turned, tile) * wts[1],
                ]
            else:
                pair = [zero] * ang_dev
            for i in range(ang_dev):
                rolled = pltpu.roll(pair[i], LANES - 1, 1)
                nxt = zero if after[i] is None else after[i]
                fdif[i, t + 1] = jnp.where(lane == LANES - 1, nxt, rolled) - pair[i]
                if t >= 0:
                    fval[i, t + 1] = pair[i]
                after[i] = rolled
        for i in range(ang_dev):
            a = chunk * ang_dev + i
            cosine = psm[0, a]
            sine = psm[1, a]
            center = half + shift_ref[a].astype(jnp.float32)
            ramp = lanef * cosine + rowf * sine
            least = jnp.minimum(cosine * (LANES - 1), 0.0) + jnp.minimum(
                first_row * sine, (first_row + (rows_dev - 1)) * sine
            )
            for b in range(nblocks):
                base = (b * LANES - half) * cosine + center + LANES
                low = (base + least - 0.25).astype(jnp.int32) // LANES
                low = jnp.minimum(jnp.maximum(low, 0), ntiles - 2)
                u = ramp + (base - (low * LANES).astype(jnp.float32))
                bin_lo = u.astype(jnp.int32)
                frac = u - bin_lo.astype(jnp.float32)
                where = jnp.bitwise_and(bin_lo, LANES - 1)
                first = bin_lo < LANES

                def pick(ref):
                    return jnp.where(
                        first,
                        jnp.take_along_axis(ref[i, low], where, axis=1, mode="promise_in_bounds"),
                        jnp.take_along_axis(
                            ref[i, low + 1], where, axis=1, mode="promise_in_bounds"
                        ),
                    )

                acc[b] += pick(fval) + frac * pick(fdif)

    def corner(k):
        relay_x(k).wait_recv()
        relay_y(k).wait_recv()
        project(at(diag, k))

    project(me)

    @pl.loop(1, depth)
    def _(k):
        relay(k)
        project(at(me, k))
        project(at(xpeer, k - 1))
        project(at(ypeer, k - 1))

    project(at(xpeer, depth - 1))
    project(at(ypeer, depth - 1))

    @pl.loop(0, depth)
    def _(k):
        corner(k)

    for b in range(nblocks):
        done = acc[b]
        for r in range(rows_dev):
            out_ref[r, :, b * LANES : (b + 1) * LANES] = done[r * slices : (r + 1) * slices]

    @pl.loop(0, depth)
    def _(k):
        xcopy(k).wait_send()
        ycopy(k).wait_send()
        relay_x(k).wait_send()
        relay_y(k).wait_send()

    @pl.loop(1, depth)
    def _(k):
        zcopy(k).wait_send()


def body(sinogram, jitter, shift):
    width = lax.axis_size("blk")
    ang_dev, slices, bins = sinogram.shape
    angles = shift.shape[0]
    rows_dev = SUBS // slices
    assert ang_dev == 2 and ang_dev * slices == SUBS and LANES % angles == 0
    assert width % PLANE == 0 and bins % (2 * BLOCK) == 0
    depth = width // PLANE
    ntiles = bins // LANES + 3
    vmem = pl.BlockSpec(memory_space=pltpu.VMEM)
    smem = pl.BlockSpec(memory_space=pltpu.SMEM)
    dma = pltpu.SemaphoreType.DMA
    slab = jnp.asarray(ramp_slab(bins))
    return pl.pallas_call(
        functools.partial(kernel, width),
        out_shape=pltpu.VMEM((rows_dev, slices, bins), jnp.float32),
        in_specs=[vmem, smem, vmem, pl.BlockSpec(memory_space=pl.ANY)],
        out_specs=vmem,
        scratch_shapes=[
            pltpu.VMEM(slab.shape, jnp.bfloat16),
            pltpu.VMEM((width, 2, 2 * SUBS, bins // 4), jnp.bfloat16),
            pltpu.VMEM((SUBS, LANES), jnp.float32),
            pltpu.VMEM((width, SUBS, LANES), jnp.float32),
            pltpu.VMEM((SUBS, LANES), jnp.float32),
            pltpu.SMEM((SUBS, LANES), jnp.float32),
            pltpu.VMEM((ang_dev, ntiles, SUBS, LANES), jnp.float32),
            pltpu.VMEM((ang_dev, ntiles, SUBS, LANES), jnp.float32),
            pltpu.VMEM((bins // LANES, SUBS, LANES), jnp.float32),
            dma((2,)),
            dma((width,)),
            dma((width,)),
            dma((depth,)),
            dma((depth,)),
            dma((depth,)),
            dma((depth,)),
            dma((depth,)),
            dma((depth,)),
            dma((2, depth)),
            dma((2, depth)),
        ],
        compiler_params=pltpu.CompilerParams(collective_id=0, has_side_effects=True),
    )(jitter.reshape(1, ang_dev), shift, sinogram, slab)


def solution(mesh):
    in_specs = (P("blk", "slab", None), P("blk"), P())
    out_specs = P("blk", "slab", None)
    return jax.shard_map(body, mesh=mesh, in_specs=in_specs, out_specs=out_specs, check_vma=False)
```

```python
import functools
import math

import jax
import jax.numpy as jnp
import numpy as np
from jax import lax
from jax.experimental import pallas as pl
from jax.experimental.pallas import tpu as pltpu
from jax.sharding import PartitionSpec as P

LANES = 128
SUBS = 8
BLOCK = 256
PLANE = 4
MESH = pl.DeviceIdType.MESH


def ramp_slab(bins):
    span = 2 * bins - BLOCK
    offsets = (
        np.arange(span, dtype=np.int32)[None, :]
        - np.int32(bins - BLOCK)
        - np.arange(BLOCK, dtype=np.int32)[:, None]
    )
    safe = np.where(offsets == 0, 1, offsets).astype(np.float32)
    odd_part = np.where(
        offsets % 2 != 0, np.float32(-1.0) / (np.float32(math.pi**2) * safe * safe), np.float32(0)
    )
    return np.where(offsets == 0, np.float32(0.25), odd_part).astype(jnp.bfloat16)


def kernel(
    width,
    jit_ref,
    shift_ref,
    sino_ref,
    slab_hbm,
    out_ref,
    slab,
    chunks,
    jmsg,
    jall,
    pvec,
    psm,
    tvec,
    tsm,
    fval,
    fdif,
    acc,
    lsem,
    sj,
    rj,
    sz,
    rz,
    sx,
    rx,
    sy,
    ry,
    sd,
    rd,
):
    me = lax.axis_index("blk")
    ang_dev, slices, bins = sino_ref.shape
    rows_dev = out_ref.shape[0]
    angles = width * ang_dev
    nrows = width * rows_dev
    nblocks = bins // LANES
    ntiles = fval.shape[2]
    depth = width // PLANE
    px, py = me % 2, (me // 2) % 2
    xpeer = me + 1 - 2 * px
    ypeer = me + 2 - 4 * py
    diag = me + 1 - 2 * px + 2 - 4 * py

    def remote(src, dst, send, recv, dev):
        return pltpu.make_async_remote_copy(
            src_ref=src,
            dst_ref=dst,
            send_sem=send,
            recv_sem=recv,
            device_id={"blk": dev},
            device_id_type=MESH,
        )

    def at(dev, k):
        return (dev + width - PLANE * k) % width

    def zcopy(k):
        return remote(
            chunks.at[me], chunks.at[me], sz.at[k], rz.at[k], (me + PLANE * k) % width
        )

    def xcopy(k):
        c = at(me, k)
        return remote(chunks.at[c], chunks.at[c], sx.at[k], rx.at[k], xpeer)

    def ycopy(k):
        c = at(me, k)
        return remote(chunks.at[c], chunks.at[c], sy.at[k], ry.at[k], ypeer)

    def relay_x(k):
        c = at(xpeer, k)
        return remote(
            chunks.at[c, 0], chunks.at[c, 0], sd.at[0, k], rd.at[0, k], ypeer
        )

    def relay_y(k):
        c = at(ypeer, k)
        return remote(
            chunks.at[c, 1], chunks.at[c, 1], sd.at[1, k], rd.at[1, k], xpeer
        )

    def jcopy(i):
        return remote(jmsg, jall.at[me], sj.at[i], rj.at[i], (me + i) % width)

    def relay(k):
        xcopy(k).wait_recv()
        relay_x(k).start()
        ycopy(k).wait_recv()
        relay_y(k).start()

    barrier = pltpu.get_barrier_semaphore()

    @pl.loop(1, width)
    def _(i):
        pl.semaphore_signal(
            barrier, inc=1, device_id={"blk": (me + i) % width}, device_id_type=MESH
        )

    load = pltpu.make_async_copy(slab_hbm, slab, lsem.at[0])
    load.start()

    lane = lax.broadcasted_iota(jnp.int32, (SUBS, LANES), 1)
    sub = lax.broadcasted_iota(jnp.int32, (SUBS, LANES), 0)
    lanef = lane.astype(jnp.float32)
    mine = (lane[:1] % angles) - me * ang_dev
    msg = jnp.zeros((1, LANES), jnp.float32)
    for i in range(ang_dev):
        msg = jnp.where(mine == i, jit_ref[0:1, i : i + 1].astype(jnp.float32), msg)
    jmsg[...] = msg
    jall[me] = msg
    zero = jnp.zeros((SUBS, LANES), jnp.float32)
    for i in range(ang_dev):
        for slot in range(fval.shape[0]):
            for t in [0] + list(range(nblocks + 1, ntiles)):
                fval[slot, i, t] = zero
                fdif[slot, i, t] = zero
    for b in range(nblocks):
        acc[b] = zero

    nb = bins // BLOCK
    flat = jnp.concatenate(
        [sino_ref[i].astype(jnp.float32) for i in range(ang_dev)], axis=0
    )
    lhs = jnp.concatenate(
        [flat[:, i * BLOCK : (i + 1) * BLOCK] for i in range(nb)], axis=0
    ).astype(jnp.bfloat16)
    load.wait()
    total = [None] * nb
    for d in range(2 * nb - 1):
        prod = jnp.dot(
            lhs, slab[:, d * BLOCK : (d + 1) * BLOCK], preferred_element_type=jnp.float32
        )
        for i in range(nb):
            j = d - (nb - 1) + i
            if 0 <= j < nb:
                piece = prod[i * SUBS : (i + 1) * SUBS]
                total[j] = piece if total[j] is None else total[j] + piece
    row = jnp.concatenate(total, axis=1)
    quarter = bins // 4
    for h in range(2):
        chunks[me, h] = jnp.concatenate(
            [row[:, (2 * h + q) * quarter : (2 * h + q + 1) * quarter] for q in range(2)], axis=0
        ).astype(jnp.bfloat16)

    pl.semaphore_wait(barrier, width - 1)

    @pl.loop(1, width)
    def _(i):
        jcopy(i).start()

    @pl.loop(1, depth)
    def _(k):
        zcopy(k).start()

    xcopy(0).start()
    ycopy(0).start()

    relay(0)

    @pl.loop(1, depth)
    def _(k):
        zcopy(k).wait_recv()
        xcopy(k).start()
        ycopy(k).start()

    half = (bins - 1) / 2
    first_row = (me * rows_dev).astype(jnp.float32) - (nrows - 1) / 2
    moved = jnp.zeros((SUBS, LANES), jnp.int32)
    for a in range(angles):
        moved = jnp.where(lane == a, shift_ref[a], moved)
    center = half + moved.astype(jnp.float32) + LANES

    @pl.loop(1, width)
    def _(i):
        jcopy(i).wait()

    jit = jall[0]
    for i in range(1, width):
        jit = jit + jall[i]
    jit = jnp.broadcast_to(jit, (SUBS, LANES))
    ahead = pltpu.roll(jit, LANES - 1, 1)
    behind = pltpu.roll(jit, 1, 1)
    weight = (1.0 + (ahead - behind) * 1.5) * (4.0 / math.sqrt(angles))
    theta = ((lane % angles).astype(jnp.float32) + jit) * math.pi / angles
    cosine = jnp.cos(theta)
    sine = jnp.sin(theta)
    least = jnp.minimum(cosine * (LANES - 1), 0.0) + jnp.minimum(
        first_row * sine, (first_row + (rows_dev - 1)) * sine
    )
    for g in range(nblocks // SUBS):
        group = slice(g * SUBS, (g + 1) * SUBS)
        start = ((sub + g * SUBS) * LANES).astype(jnp.float32) - half
        base = start * cosine + center
        low = (base + least - 0.25).astype(jnp.int32) // LANES
        low = jnp.minimum(jnp.maximum(low, 0), ntiles - 2)
        tvec[group] = low
        pvec[group] = base - (low * LANES).astype(jnp.float32)
    pvec[nblocks:] = jnp.where(sub == 0, cosine, jnp.where(sub == 1, sine, weight))
    moves = [
        pltpu.make_async_copy(pvec, psm, lsem.at[1]),
        pltpu.make_async_copy(tvec, tsm, lsem.at[2]),
    ]
    for move in moves:
        move.start()
    for move in moves:
        move.wait()

    rowf = (sub // slices).astype(jnp.float32) + first_row
    low_half = sub < slices

    def spread(chunk, slot):
        after = [None] * ang_dev
        wts = [psm[nblocks + 2, chunk * ang_dev + i] for i in range(ang_dev)]
        for t in range(nblocks - 1, -2, -1):
            if t >= 0:
                h, q, k = t // (nblocks // 2), (t // (nblocks // 4)) % 2, t % (nblocks // 4)
                tile = chunks[
                    chunk, h, q * SUBS : (q + 1) * SUBS, k * LANES : (k + 1) * LANES
                ].astype(jnp.float32)
                turned = pltpu.roll(tile, slices, 0)
                pair = [
                    jnp.where(low_half, tile, turned) * wts[0],
                    jnp.where(low_half, turned, tile) * wts[1],
                ]
            else:
                pair = [zero] * ang_dev
            for i in range(ang_dev):
                rolled = pltpu.roll(pair[i], LANES - 1, 1)
                nxt = zero if after[i] is None else after[i]
                fdif[slot, i, t + 1] = jnp.where(lane == LANES - 1, nxt, rolled) - pair[i]
                if t >= 0:
                    fval[slot, i, t + 1] = pair[i]
                after[i] = rolled

    def add_up(chunk, slot, sums):
        for i in range(ang_dev):
            a = chunk * ang_dev + i
            ramp = lanef * psm[nblocks, a] + rowf * psm[nblocks + 1, a]
            for b in range(nblocks):
                low = tsm[b, a]
                u = ramp + psm[b, a]
                bin_lo = u.astype(jnp.int32)
                frac = u - bin_lo.astype(jnp.float32)
                where = jnp.bitwise_and(bin_lo, LANES - 1)
                first = bin_lo < LANES

                def pick(ref):
                    return jnp.where(
                        first,
                        jnp.take_along_axis(ref[slot, i, low], where, axis=1, mode="promise_in_bounds"),
                        jnp.take_along_axis(
                            ref[slot, i, low + 1], where, axis=1, mode="promise_in_bounds"
                        ),
                    )

                got = pick(fval) + frac * pick(fdif)
                sums[b] = got if sums[b] is None else sums[b] + got

    def project(*group):
        for slot, chunk in enumerate(group):
            spread(chunk, slot)
        sums = [None] * nblocks
        for slot, chunk in enumerate(group):
            add_up(chunk, slot, sums)
        for b in range(nblocks):
            acc[b] += sums[b]

    def corner(k):
        relay_x(k).wait_recv()
        relay_y(k).wait_recv()

    project(me)

    @pl.loop(1, depth)
    def _(k):
        relay(k)
        project(at(me, k), at(xpeer, k - 1), at(ypeer, k - 1))

    corner(0)
    project(at(xpeer, depth - 1), at(ypeer, depth - 1), at(diag, 0))

    @pl.loop(1, depth - 1)
    def _(k):
        corner(k)
        project(at(diag, k))

    corner(depth - 1)
    project(at(diag, depth - 1))

    for b in range(nblocks):
        done = acc[b]
        for r in range(rows_dev):
            out_ref[r, :, b * LANES : (b + 1) * LANES] = done[r * slices : (r + 1) * slices]

    @pl.loop(0, depth)
    def _(k):
        xcopy(k).wait_send()
        ycopy(k).wait_send()
        relay_x(k).wait_send()
        relay_y(k).wait_send()

    @pl.loop(1, depth)
    def _(k):
        zcopy(k).wait_send()


def body(sinogram, jitter, shift):
    width = lax.axis_size("blk")
    ang_dev, slices, bins = sinogram.shape
    angles = shift.shape[0]
    rows_dev = SUBS // slices
    assert ang_dev == 2 and ang_dev * slices == SUBS and LANES % angles == 0
    assert width % PLANE == 0 and bins % (2 * BLOCK) == 0
    depth = width // PLANE
    ntiles = bins // LANES + 3
    vmem = pl.BlockSpec(memory_space=pltpu.VMEM)
    smem = pl.BlockSpec(memory_space=pltpu.SMEM)
    dma = pltpu.SemaphoreType.DMA
    slab = jnp.asarray(ramp_slab(bins))
    return pl.pallas_call(
        functools.partial(kernel, width),
        out_shape=pltpu.VMEM((rows_dev, slices, bins), jnp.float32),
        in_specs=[vmem, smem, vmem, pl.BlockSpec(memory_space=pl.ANY)],
        out_specs=vmem,
        scratch_shapes=[
            pltpu.VMEM(slab.shape, jnp.bfloat16),
            pltpu.VMEM((width, 2, 2 * SUBS, bins // 4), jnp.bfloat16),
            pltpu.VMEM((1, LANES), jnp.float32),
            pltpu.VMEM((width, 1, LANES), jnp.float32),
            pltpu.VMEM((bins // LANES + SUBS, LANES), jnp.float32),
            pltpu.SMEM((bins // LANES + SUBS, LANES), jnp.float32),
            pltpu.VMEM((bins // LANES, LANES), jnp.int32),
            pltpu.SMEM((bins // LANES, LANES), jnp.int32),
            pltpu.VMEM((3, ang_dev, ntiles, SUBS, LANES), jnp.float32),
            pltpu.VMEM((3, ang_dev, ntiles, SUBS, LANES), jnp.float32),
            pltpu.VMEM((bins // LANES, SUBS, LANES), jnp.float32),
            dma((3,)),
            dma((width,)),
            dma((width,)),
            dma((depth,)),
            dma((depth,)),
            dma((depth,)),
            dma((depth,)),
            dma((depth,)),
            dma((depth,)),
            dma((2, depth)),
            dma((2, depth)),
        ],
        compiler_params=pltpu.CompilerParams(collective_id=0, has_side_effects=True),
    )(jitter.reshape(1, ang_dev), shift, sinogram, slab)


def solution(mesh):
    in_specs = (P("blk", "slab", None), P("blk"), P())
    out_specs = P("blk", "slab", None)
    return jax.shard_map(body, mesh=mesh, in_specs=in_specs, out_specs=out_specs, check_vma=False)
```
